32 devices in a mesh: dp: 4 (over y, core), tm: 8 (over z, x).
Axes of the slice: x: 2, y: 2, z: 4, core: 2. Of those that a mesh axis runs over, the one named last changes fastest.
Arguments:
- latents: bfloat16 [4, 64, 64, 1280], P('dp', 'tm'), may hold values from -6 to 6
- conv_weight: bfloat16 [1280, 3840], replicated, may hold values from -0.09375 to 0.09375
- qkv_weight: bfloat16 [1280, 1920], replicated, may hold values from -2 to 2
- out_weight: bfloat16 [640, 1280], replicated, may hold values from -0.25 to 0.25
- out_cotangent: bfloat16 [4, 32, 64, 1280], P('dp', 'tm'), may hold values from -6 to 6
Outputs:
- input_grad: bfloat16 [4, 64, 64, 1280], P('dp', 'tm')
- conv_grad: bfloat16 [1280, 3840], P('tm')
- qkv_grad: bfloat16 [1280, 1920], P('tm')
- proj_grad: bfloat16 [640, 1280], P('tm')
The draws below stay inside these ranges and needn't reach their ends.
All inputs are finite; a program needn't handle non-finite values.
Results may differ from the reference program's by a relative error of at most 0.04.
Values may be sent and summed in bfloat16 or wider, within the bound.
A program may use at most 192 MiB of HBM per device.

```python
import math
import jax
import jax.numpy as jnp
from jax import lax

CH = 1280
HEADS = 10
HEAD = 64
S = 64
HD = 640
FRAMES = 64
OUTF = 32
VIDEOS = 4


def draw_qkv_weight(key, part):
    first_key = jax.random.fold_in(jax.random.fold_in(key, 17), 0)
    base = jax.random.normal(first_key, (CH, 3 * HD), jnp.float32) / math.sqrt(CH)
    result = base
    return result.astype(jnp.bfloat16)


def with_spikes(array, own_key, source, target, shards_of, factor):
    def block_of(axis_at):
        return (jnp.arange(array.shape[axis_at]) // (array.shape[axis_at] // shards_of)).reshape((-1,) + (1,) * (array.ndim - 1 - axis_at))

    first = jax.random.permutation(own_key, shards_of)[block_of(target)]
    second = (block_of(target) + shards_of // 2) % shards_of
    return jnp.where((block_of(source) == first) | (block_of(source) == second), factor * array, array)


def levels(own_key, shape, cuts, least, largest):
    def one(position, shards_of):
        draws = jax.random.uniform(jax.random.fold_in(jax.random.fold_in(own_key, 6), position), (shards_of,), jnp.float32, least / len(cuts), largest / len(cuts))
        return jnp.repeat(jnp.exp(draws), shape[position] // shards_of).reshape((-1,) + (1,) * (len(shape) - position - 1))

    factor_of = one(*cuts[0])
    for cut in cuts[1:]:
        factor_of = factor_of * one(*cut)
    return factor_of


def bell_draw(key, dims, scale, reach, cuts=(), dtype=jnp.bfloat16):
    values = jax.random.normal(key, dims, jnp.float32) * scale
    if len(cuts) > 0:
        values = levels(key, dims, cuts, -0.22, 0.18) * values
    return jnp.clip(values, min=-reach, max=reach).astype(dtype)


def gaussian_with(own_key, dims, deviation, most, shards, heavy, kind=jnp.bfloat16):
    drawn = deviation * jax.random.normal(own_key, dims, jnp.float32)
    if shards:
        drawn = drawn * levels(own_key, dims, shards, -0.22, 0.18)
    return jnp.clip(with_spikes(drawn, jax.random.fold_in(own_key, 3), *heavy), -most, most).astype(kind)


def setup_inputs(seed: int = 0) -> dict:
    splits = jax.random.split(jax.random.key(seed), 6)
    return {
        "latents": gaussian_with(splits[0], (VIDEOS, FRAMES, S, CH), 1.0, 6.0, ((0, 4), (1, 8)), (1, 3, 8, 2.0)),
        "conv_weight": bell_draw(splits[1], (CH, 3 * CH), (3 * CH) ** -0.5, 0.09375),
        "qkv_weight": draw_qkv_weight(jax.random.fold_in(splits[5], 71), 0),
        "out_weight": bell_draw(splits[3], (HD, CH), HD ** -0.5, 0.25),
        "out_cotangent": bell_draw(splits[4], (VIDEOS, OUTF, S, CH), 1.0, 6.0, ((0, 4), (1, 8))),
    }


EPSILON = 1e-05

def rounded(values):
    return lax.optimization_barrier(values.astype(jnp.bfloat16))

def dot_rows(left_side, right_side):
    return jnp.dot(left_side, right_side, preferred_element_type=jnp.float32)

def attend_location(packed):
    qkv_one, grad_one = packed
    width = qkv_one.shape[-1] // 3
    shape = qkv_one.shape[:2] + (HEADS, HEAD)
    queries = qkv_one[..., :width].reshape(shape).astype(jnp.float32)
    keys = qkv_one[..., width:2 * width].reshape(shape).astype(jnp.float32)
    values = qkv_one[..., 2 * width:].reshape(shape).astype(jnp.float32)
    grad_att = grad_one.reshape(shape).astype(jnp.float32)
    scores = jnp.einsum('vqhd,vkhd->vhqk', queries, keys) / math.sqrt(HEAD)
    highest = lax.optimization_barrier(jnp.max(scores, axis=-1, keepdims=True))
    expo = jnp.exp(scores - highest)
    probs = expo / lax.optimization_barrier(jnp.sum(expo, axis=-1, keepdims=True))
    probs_b = rounded(probs).astype(jnp.float32)
    attended = rounded(jnp.einsum('vhqk,vkhd->vqhd', probs_b, values))
    grad_values = rounded(jnp.einsum('vhqk,vqhd->vkhd', probs_b, grad_att))
    grad_probs = jnp.einsum('vqhd,vkhd->vhqk', grad_att, values)
    row_delta = lax.optimization_barrier(jnp.sum(grad_att * attended.astype(jnp.float32), axis=-1))
    row_delta = jnp.transpose(row_delta, (0, 2, 1))[..., None]
    grad_scores = rounded(probs * (grad_probs - row_delta) / math.sqrt(HEAD)).astype(jnp.float32)
    grad_queries = rounded(jnp.einsum('vhqk,vkhd->vqhd', grad_scores, keys))
    grad_keys = rounded(jnp.einsum('vhqk,vqhd->vkhd', grad_scores, queries))
    flat_shape = qkv_one.shape[:2] + (width,)
    grad_qkv = jnp.concatenate([grad_queries.reshape(flat_shape), grad_keys.reshape(flat_shape), grad_values.reshape(flat_shape)], axis=-1)
    return (attended.reshape(flat_shape), grad_qkv)

def reference(latents, conv_weight, qkv_weight, out_weight, out_cotangent):
    videos, frames, places, width = latents.shape
    half = frames // 2
    attn_width = out_weight.shape[0]
    split = latents.reshape(videos, half, 2, places, width)
    even_frames = split[:, :, 0]
    odd_frames = split[:, :, 1]
    prev_frames = jnp.concatenate([jnp.zeros_like(odd_frames[:, :1]), odd_frames[:, :-1]], axis=1)
    total_rows = videos * half * places

    def as_rows(values):
        return values.reshape(total_rows, values.shape[-1])
    tap_zero = conv_weight[:, :width]
    tap_one = conv_weight[:, width:2 * width]
    tap_two = conv_weight[:, 2 * width:]
    hidden = rounded(dot_rows(as_rows(prev_frames), tap_zero) + dot_rows(as_rows(even_frames), tap_one) + dot_rows(as_rows(odd_frames), tap_two))
    hidden_f = hidden.astype(jnp.float32)
    centred = hidden_f - lax.optimization_barrier(jnp.mean(hidden_f, axis=-1, keepdims=True))
    inv_std = lax.rsqrt(lax.optimization_barrier(jnp.mean(centred * centred, axis=-1, keepdims=True)) + EPSILON)
    unit_rows = centred * inv_std
    normed = rounded(unit_rows)
    qkv_rows = rounded(dot_rows(normed, qkv_weight))
    grad_rows = as_rows(out_cotangent)
    grad_att = rounded(dot_rows(grad_rows, out_weight.T))
    qkv_loc = jnp.transpose(qkv_rows.reshape(videos, half, places, 3 * attn_width), (2, 0, 1, 3))
    grad_loc = jnp.transpose(grad_att.reshape(videos, half, places, attn_width), (2, 0, 1, 3))
    attended_loc, grad_qkv_loc = lax.map(attend_location, (qkv_loc, grad_loc))
    attended = jnp.transpose(attended_loc, (1, 2, 0, 3)).reshape(total_rows, attn_width)
    grad_qkv = jnp.transpose(grad_qkv_loc, (1, 2, 0, 3)).reshape(total_rows, 3 * attn_width)
    grad_normed = dot_rows(grad_qkv, qkv_weight.T)
    correction = grad_normed - lax.optimization_barrier(jnp.mean(grad_normed, axis=-1, keepdims=True)) - unit_rows * lax.optimization_barrier(jnp.mean(grad_normed * unit_rows, axis=-1, keepdims=True))
    grad_hidden = rounded(grad_rows.astype(jnp.float32) + inv_std * correction)
    grad_four = grad_hidden.reshape(videos, half, places, width)
    grad_next = jnp.concatenate([grad_four[:, 1:], jnp.zeros_like(grad_four[:, :1])], axis=1)
    grad_even = dot_rows(grad_hidden, tap_one.T).astype(jnp.bfloat16)
    grad_odd = (dot_rows(grad_hidden, tap_two.T) + dot_rows(as_rows(grad_next), tap_zero.T)).astype(jnp.bfloat16)
    input_grad = jnp.stack([grad_even.reshape(videos, half, places, width), grad_odd.reshape(videos, half, places, width)], axis=2).reshape(latents.shape)
    grad_scale = 1.0 / math.sqrt(total_rows)
    conv_terms = jnp.concatenate([dot_rows(as_rows(prev_frames).T, grad_hidden), dot_rows(as_rows(even_frames).T, grad_hidden), dot_rows(as_rows(odd_frames).T, grad_hidden)], axis=1)
    conv_grad = (conv_terms * grad_scale).astype(jnp.bfloat16)
    qkv_grad = (dot_rows(normed.T, grad_qkv) * grad_scale).astype(jnp.bfloat16)
    proj_grad = (dot_rows(attended.T, grad_rows) * grad_scale).astype(jnp.bfloat16)
    return (input_grad, conv_grad, qkv_grad, proj_grad)
```

```python
import functools
import math

import jax
import jax.numpy as jnp
from jax import lax
from jax.experimental import pallas as pl
from jax.experimental.pallas import tpu as pltpu
from jax.sharding import PartitionSpec as P

HEADS = 10
HEAD = 64


EPSILON = 1e-05


def from_behind(shard, axis, by):
    devices = lax.axis_size(axis)
    pairs = [(i, i + by) for i in range(devices) if 0 <= i + by < devices]
    return lax.ppermute(shard, axis, pairs)


def swap(shard, axis, bit):
    devices = lax.axis_size(axis)
    return lax.ppermute(shard, axis, [(i, i ^ (1 << bit)) for i in range(devices)])


def bit_of(axis, bit):
    return (lax.axis_index(axis) >> bit) & 1


def dot_rows(left_side, right_side):
    return jnp.dot(left_side, right_side, preferred_element_type=jnp.float32)


def dot_rows_t(left_side, right_side):
    return lax.dot_general(
        left_side, right_side, (((1,), (1,)), ((), ())), preferred_element_type=jnp.float32
    )


def dot_columns(left_side, right_side):
    return lax.dot_general(
        left_side, right_side, (((0,), (0,)), ((), ())), preferred_element_type=jnp.float32
    )


def attention_kernel(loc, width, packed_ref, result_ref):
    rows = packed_ref.shape[0]
    row_at = lax.broadcasted_iota(jnp.int32, (rows, rows), 0)
    column_at = lax.broadcasted_iota(jnp.int32, (rows, rows), 1)
    same = (row_at % loc) == (column_at % loc)
    lane = lax.broadcasted_iota(jnp.int32, (rows, 2 * HEAD), 1)
    scale = 1.0 / math.sqrt(HEAD)
    for pair in range(width // (2 * HEAD)):
        first = pair * 2 * HEAD
        q = packed_ref[:, first : first + 2 * HEAD]
        k = packed_ref[:, width + first : width + first + 2 * HEAD]
        v = packed_ref[:, 2 * width + first : 2 * width + first + 2 * HEAD]
        g = packed_ref[:, 3 * width + first : 3 * width + first + 2 * HEAD]
        zero = jnp.zeros_like(q)
        grad_q = grad_k = grad_v = attended = None
        kept = []
        for head in range(2):
            mine = (lane >= HEAD) if head else (lane < HEAD)
            q_h = jnp.where(mine, q, zero)
            v_h = jnp.where(mine, v, zero)
            g_h = jnp.where(mine, g, zero)
            scores = jnp.where(same, dot_rows_t(q_h, k) * scale, -1e30)
            expo = jnp.exp(scores - jnp.max(scores, axis=1, keepdims=True))
            probs = expo * (1.0 / jnp.sum(expo, axis=1, keepdims=True))
            probs_b = probs.astype(jnp.bfloat16)
            part = dot_rows(probs_b, v_h)
            attended = part if attended is None else attended + part
            part = dot_columns(probs_b, g_h)
            grad_v = part if grad_v is None else grad_v + part
            grad_probs = dot_rows_t(g_h, v)
            kept.append((mine, q_h, probs, grad_probs))
        attended_b = attended.astype(jnp.bfloat16)
        product = g.astype(jnp.float32) * attended_b.astype(jnp.float32)
        for mine, q_h, probs, grad_probs in kept:
            k_h = jnp.where(mine, k, zero)
            delta = jnp.sum(jnp.where(mine, product, 0.0), axis=1, keepdims=True)
            grad_scores = (probs * (grad_probs - delta) * scale).astype(jnp.bfloat16)
            part = dot_rows(grad_scores, k_h)
            grad_q = part if grad_q is None else grad_q + part
            part = dot_columns(grad_scores, q_h)
            grad_k = part if grad_k is None else grad_k + part
        result_ref[:, first : first + 2 * HEAD] = grad_q.astype(jnp.bfloat16)
        result_ref[:, width + first : width + first + 2 * HEAD] = grad_k.astype(jnp.bfloat16)
        result_ref[:, 2 * width + first : 2 * width + first + 2 * HEAD] = grad_v.astype(
            jnp.bfloat16
        )
        result_ref[:, 3 * width + first : 3 * width + first + 2 * HEAD] = attended_b


def attention(packed, loc, width):
    rows = packed.shape[0]
    return pl.pallas_call(
        functools.partial(attention_kernel, loc, width),
        out_shape=jax.ShapeDtypeStruct(packed.shape, jnp.bfloat16),
        in_specs=[pl.BlockSpec(memory_space=pltpu.VMEM)],
        out_specs=pl.BlockSpec(memory_space=pltpu.VMEM),
        compiler_params=pltpu.CompilerParams(vmem_limit_bytes=40 * 1024 * 1024),
        cost_estimate=pl.CostEstimate(
            flops=14 * HEADS * rows * rows * 2 * HEAD,
            bytes_accessed=2 * packed.size * 2,
            transcendentals=HEADS * rows * rows,
        ),
    )(packed)


def halve(array, position, axis, bit):
    mine = bit_of(axis, bit)
    away = lax.dynamic_index_in_dim(array, 1 - mine, position, keepdims=False)
    stay = lax.dynamic_index_in_dim(array, mine, position, keepdims=False)
    came = swap(away, axis, bit)
    return (stay.astype(jnp.float32) + came.astype(jnp.float32)).astype(jnp.bfloat16)


def join(array, axis, bit, position):
    came = swap(array, axis, bit)
    first = bit_of(axis, bit) == 0
    return jnp.concatenate(
        [jnp.where(first, array, came), jnp.where(first, came, array)], axis=position
    )


def sum_over_devices(share, bits, y_first, scale):
    if y_first:
        share = halve(share, bits + 1, "dp", 1)
        share = halve(share, bits, "tm", 0)
    else:
        share = halve(share, bits, "tm", 0)
        share = halve(share, bits, "dp", 1)
    for bit in range(1, bits):
        share = halve(share, bits - bit, "tm", bit)
    share = (share.astype(jnp.float32) * scale).astype(jnp.bfloat16)
    return join(share, "dp", 1, 1)


def local(latents, conv_weight, qkv_weight, out_weight, out_cotangent):
    videos, frames, places, width = latents.shape
    half = frames // 2
    attn_width = out_weight.shape[0]
    dp_count = lax.axis_size("dp")
    tm_count = lax.axis_size("tm")
    bits = tm_count.bit_length() - 1
    loc = places // tm_count
    rows = half * places
    core = bit_of("dp", 0)

    def as_rows(values):
        return values.reshape(rows, values.shape[-1])

    def own_half(values, which):
        size = values.shape[-1] // 2
        return lax.dynamic_slice_in_dim(values, which * size, size, axis=values.ndim - 1)

    split = latents.reshape(half, 2, tm_count, loc, width)
    rim_input = from_behind(split[half - 1, 1], "tm", 1)
    split = jnp.transpose(split, (1, 2, 0, 3, 4))
    even_frames, odd_frames = split[0], split[1]
    prev_frames = jnp.concatenate([rim_input[:, None], odd_frames[:, : half - 1]], axis=1)
    cotangent_rows = as_rows(
        jnp.transpose(out_cotangent.reshape(half, tm_count, loc, width), (1, 0, 2, 3))
    )

    tap_zero = conv_weight[:, :width]
    tap_one = conv_weight[:, width : 2 * width]
    tap_two = conv_weight[:, 2 * width :]
    prev_rows = as_rows(prev_frames)
    even_rows = as_rows(even_frames)
    odd_rows = as_rows(odd_frames)
    conv_left = jnp.concatenate([prev_rows, even_rows, odd_rows], axis=1)
    conv_left_other = swap(conv_left, "dp", 0)
    cot_half = own_half(cotangent_rows, core)
    cot_half_other = swap(own_half(cotangent_rows, 1 - core), "dp", 0)

    grad_att = dot_rows_t(cotangent_rows, out_weight).astype(jnp.bfloat16)
    hidden = (
        dot_rows(prev_rows, tap_zero) + dot_rows(even_rows, tap_one) + dot_rows(odd_rows, tap_two)
    ).astype(jnp.bfloat16)
    hidden_f = hidden.astype(jnp.float32)
    centred = hidden_f - jnp.mean(hidden_f, axis=-1, keepdims=True)
    inv_std = lax.rsqrt(jnp.mean(centred * centred, axis=-1, keepdims=True) + EPSILON)
    unit_rows = centred * inv_std
    normed = unit_rows.astype(jnp.bfloat16)
    normed_other = swap(normed, "dp", 0)
    qkv_rows = dot_rows(normed, qkv_weight).astype(jnp.bfloat16)

    outgoing = jnp.concatenate([qkv_rows, grad_att], axis=1).reshape(tm_count, half * loc, -1)
    packed = lax.all_to_all(outgoing, "tm", split_axis=0, concat_axis=0, tiled=True)
    result = attention(packed.reshape(rows, 4 * attn_width), loc, attn_width)
    result = lax.all_to_all(
        result.reshape(tm_count, half * loc, 4 * attn_width),
        "tm",
        split_axis=0,
        concat_axis=0,
        tiled=True,
    ).reshape(rows, 4 * attn_width)
    grad_qkv = result[:, : 3 * attn_width]
    attended = result[:, 3 * attn_width :]

    grad_scale = 1.0 / math.sqrt(dp_count * tm_count * rows)

    def by_bits(share, taps, parts):
        channels = share.shape[0] // taps
        size = channels // tm_count // math.prod(parts)
        return share.reshape((taps,) + (2,) * bits + parts + (size, share.shape[1]))

    def summed(share, taps):
        share = by_bits(share, taps, (2, 2))
        ahead = lax.index_in_dim(share, 0, bits + 1, keepdims=False)
        behind = lax.index_in_dim(share, 1, bits + 1, keepdims=False)
        return jnp.concatenate(
            [
                sum_over_devices(ahead, bits, False, grad_scale),
                sum_over_devices(behind, bits, True, grad_scale),
            ],
            axis=1,
        )

    attended_other = swap(attended, "dp", 0)
    proj_share = (
        dot_columns(attended, cot_half) + dot_columns(attended_other, cot_half_other)
    ).astype(jnp.bfloat16)
    gq_half = own_half(grad_qkv, core)
    gq_half_other = swap(own_half(grad_qkv, 1 - core), "dp", 0)
    qkv_share = (dot_columns(normed, gq_half) + dot_columns(normed_other, gq_half_other)).astype(
        jnp.bfloat16
    )

    grad_normed = dot_rows_t(grad_qkv, qkv_weight)
    correction = (
        grad_normed
        - jnp.mean(grad_normed, axis=-1, keepdims=True)
        - unit_rows * jnp.mean(grad_normed * unit_rows, axis=-1, keepdims=True)
    )
    grad_hidden = (cotangent_rows.astype(jnp.float32) + inv_std * correction).astype(jnp.bfloat16)
    gh_half = own_half(grad_hidden, core)
    gh_half_other = swap(own_half(grad_hidden, 1 - core), "dp", 0)
    conv_share = (
        dot_columns(conv_left, gh_half) + dot_columns(conv_left_other, gh_half_other)
    ).astype(jnp.bfloat16)

    proj_sum = sum_over_devices(by_bits(proj_share, 1, (2,)), bits, True, grad_scale)
    qkv_sum = summed(qkv_share, 1)
    conv_sum = summed(conv_share, 3)

    grad_four = grad_hidden.reshape(tm_count, half, loc, width)
    rim_after = from_behind(grad_four[:, 0], "tm", -1)
    grad_next = jnp.concatenate([grad_four[:, 1:], rim_after[:, None]], axis=1)
    grad_even = dot_rows_t(grad_hidden, tap_one).astype(jnp.bfloat16)
    grad_odd = (dot_rows_t(grad_hidden, tap_two) + dot_rows_t(as_rows(grad_next), tap_zero)).astype(
        jnp.bfloat16
    )
    by_frame = (tm_count, half, loc, width)
    input_grad = jnp.transpose(
        jnp.stack([grad_even.reshape(by_frame), grad_odd.reshape(by_frame)], axis=0),
        (2, 0, 1, 3, 4),
    ).reshape(latents.shape)

    proj_grad = join(proj_sum[0], "dp", 0, 1)
    qkv_grad = join(qkv_sum[0], "dp", 0, 1)
    conv_both = join(conv_sum[:, :, None], "dp", 0, 2)
    conv_grad = jnp.transpose(conv_both, (1, 0, 2, 3)).reshape(conv_both.shape[1], 3 * width)
    return (input_grad, conv_grad, qkv_grad, proj_grad)


def solution(mesh):
    return jax.shard_map(
        local,
        mesh=mesh,
        in_specs=(P("dp", "tm", None, None), P(), P(), P(), P("dp", "tm", None, None)),
        out_specs=(P("dp", "tm", None, None), P("tm", None), P("tm", None), P("tm", None)),
        check_vma=False,
    )
```

```python
import functools
import math

import jax
import jax.numpy as jnp
from jax import lax
from jax.experimental import pallas as pl
from jax.experimental.pallas import tpu as pltpu
from jax.sharding import PartitionSpec as P

HEADS = 10
HEAD = 64


EPSILON = 1e-05


def from_behind(shard, axis, by):
    devices = lax.axis_size(axis)
    pairs = [(i, i + by) for i in range(devices) if 0 <= i + by < devices]
    return lax.ppermute(shard, axis, pairs)


def swap(shard, axis, mask):
    devices = lax.axis_size(axis)
    return lax.ppermute(shard, axis, [(i, i ^ mask) for i in range(devices)])


def bit_of(axis, bit):
    return (lax.axis_index(axis) >> bit) & 1


def dot_rows(left_side, right_side):
    return jnp.dot(left_side, right_side, preferred_element_type=jnp.float32)


def dot_rows_t(left_side, right_side):
    return lax.dot_general(
        left_side, right_side, (((1,), (1,)), ((), ())), preferred_element_type=jnp.float32
    )


def dot_columns(left_side, right_side):
    return lax.dot_general(
        left_side, right_side, (((0,), (0,)), ((), ())), preferred_element_type=jnp.float32
    )


def attention_kernel(loc, width, packed_ref, result_ref):
    rows = packed_ref.shape[0]
    row_at = lax.broadcasted_iota(jnp.int32, (rows, rows), 0)
    column_at = lax.broadcasted_iota(jnp.int32, (rows, rows), 1)
    same = (row_at % loc) == (column_at % loc)
    lane = lax.broadcasted_iota(jnp.int32, (rows, 2 * HEAD), 1)
    scale = 1.0 / math.sqrt(HEAD)
    for pair in range(width // (2 * HEAD)):
        first = pair * 2 * HEAD
        q = packed_ref[:, first : first + 2 * HEAD]
        k = packed_ref[:, width + first : width + first + 2 * HEAD]
        v = packed_ref[:, 2 * width + first : 2 * width + first + 2 * HEAD]
        g = packed_ref[:, 3 * width + first : 3 * width + first + 2 * HEAD]
        zero = jnp.zeros_like(q)
        grad_q = grad_k = grad_v = attended = None
        kept = []
        for head in range(2):
            mine = (lane >= HEAD) if head else (lane < HEAD)
            q_h = jnp.where(mine, q, zero)
            v_h = jnp.where(mine, v, zero)
            g_h = jnp.where(mine, g, zero)
            scores = jnp.where(same, dot_rows_t(q_h, k) * scale, -1e30)
            expo = jnp.exp(scores - jnp.max(scores, axis=1, keepdims=True))
            probs = expo * (1.0 / jnp.sum(expo, axis=1, keepdims=True))
            probs_b = probs.astype(jnp.bfloat16)
            part = dot_rows(probs_b, v_h)
            attended = part if attended is None else attended + part
            part = dot_columns(probs_b, g_h)
            grad_v = part if grad_v is None else grad_v + part
            grad_probs = dot_rows_t(g_h, v)
            kept.append((mine, q_h, probs, grad_probs))
        attended_b = attended.astype(jnp.bfloat16)
        product = g.astype(jnp.float32) * attended_b.astype(jnp.float32)
        for mine, q_h, probs, grad_probs in kept:
            k_h = jnp.where(mine, k, zero)
            delta = jnp.sum(jnp.where(mine, product, 0.0), axis=1, keepdims=True)
            grad_scores = (probs * (grad_probs - delta) * scale).astype(jnp.bfloat16)
            part = dot_rows(grad_scores, k_h)
            grad_q = part if grad_q is None else grad_q + part
            part = dot_columns(grad_scores, q_h)
            grad_k = part if grad_k is None else grad_k + part
        result_ref[:, first : first + 2 * HEAD] = grad_q.astype(jnp.bfloat16)
        result_ref[:, width + first : width + first + 2 * HEAD] = grad_k.astype(jnp.bfloat16)
        result_ref[:, 2 * width + first : 2 * width + first + 2 * HEAD] = grad_v.astype(
            jnp.bfloat16
        )
        result_ref[:, 3 * width + first : 3 * width + first + 2 * HEAD] = attended_b


def attention(packed, loc, width):
    rows = packed.shape[0]
    return pl.pallas_call(
        functools.partial(attention_kernel, loc, width),
        out_shape=jax.ShapeDtypeStruct(packed.shape, jnp.bfloat16),
        in_specs=[pl.BlockSpec(memory_space=pltpu.VMEM)],
        out_specs=pl.BlockSpec(memory_space=pltpu.VMEM),
        compiler_params=pltpu.CompilerParams(vmem_limit_bytes=40 * 1024 * 1024),
        cost_estimate=pl.CostEstimate(
            flops=14 * HEADS * rows * rows * 2 * HEAD,
            bytes_accessed=2 * packed.size * 2,
            transcendentals=HEADS * rows * rows,
        ),
    )(packed)


def add_rounded(terms, scale=None):
    total = functools.reduce(jnp.add, [term.astype(jnp.float32) for term in terms])
    return (total if scale is None else total * scale).astype(jnp.bfloat16)


def halve(share):
    mine = bit_of("tm", 0)
    away = lax.dynamic_index_in_dim(share, 1 - mine, 1, keepdims=False)
    stay = lax.dynamic_index_in_dim(share, mine, 1, keepdims=False)
    return add_rounded([stay, swap(away, "tm", 1)])


def scatter_high(share, scale):
    mine = lax.axis_index("tm") >> 1
    terms = [lax.dynamic_index_in_dim(share, mine, 0, keepdims=False)]
    for mask in range(1, share.shape[0]):
        away = lax.dynamic_index_in_dim(share, mine ^ mask, 0, keepdims=False)
        terms.append(swap(away, "tm", 2 * mask))
    return add_rounded(terms, scale)


def join(array, bit):
    came = swap(array, "dp", 1 << bit)
    first = bit_of("dp", bit) == 0
    return jnp.concatenate(
        [jnp.where(first, array, came), jnp.where(first, came, array)], axis=1
    )


def local(latents, conv_weight, qkv_weight, out_weight, out_cotangent):
    videos, frames, places, width = latents.shape
    half = frames // 2
    attn_width = out_weight.shape[0]
    dp_count = lax.axis_size("dp")
    tm_count = lax.axis_size("tm")
    high = tm_count // 2
    loc = places // tm_count
    rows = half * places
    dp_at = lax.axis_index("dp")

    def as_rows(values):
        return values.reshape(rows, values.shape[-1])

    def quarter(values, mask):
        size = values.shape[-1] // dp_count
        other = dp_at ^ mask
        which = (other & 1) * (dp_count // 2) + (other >> 1)
        return lax.dynamic_slice_in_dim(values, which * size, size, axis=values.ndim - 1)

    def all_rows(values):
        own_core = swap(values, "dp", 1)
        across = swap(values, "dp", 2)
        return [values, own_core, across, swap(across, "dp", 1)]

    def own_columns(values):
        return [quarter(values, 0)] + [
            swap(quarter(values, mask), "dp", mask) for mask in range(1, dp_count)
        ]

    def share_of(lefts, rights):
        return functools.reduce(
            jnp.add, [dot_columns(left, right) for left, right in zip(lefts, rights)]
        ).astype(jnp.bfloat16)

    split = latents.reshape(half, 2, tm_count, loc, width)
    rim_input = from_behind(split[half - 1, 1], "tm", 1)
    split = jnp.transpose(split, (1, 2, 0, 3, 4))
    even_frames, odd_frames = split[0], split[1]
    prev_frames = jnp.concatenate([rim_input[:, None], odd_frames[:, : half - 1]], axis=1)
    cotangent_rows = as_rows(
        jnp.transpose(out_cotangent.reshape(half, tm_count, loc, width), (1, 0, 2, 3))
    )

    tap_zero = conv_weight[:, :width]
    tap_one = conv_weight[:, width : 2 * width]
    tap_two = conv_weight[:, 2 * width :]
    prev_rows = as_rows(prev_frames)
    even_rows = as_rows(even_frames)
    odd_rows = as_rows(odd_frames)
    conv_left = jnp.concatenate([prev_rows, even_rows, odd_rows], axis=1)
    conv_lefts = all_rows(conv_left)
    cot_columns = own_columns(cotangent_rows)

    grad_att = dot_rows_t(cotangent_rows, out_weight).astype(jnp.bfloat16)
    hidden = (
        dot_rows(prev_rows, tap_zero) + dot_rows(even_rows, tap_one) + dot_rows(odd_rows, tap_two)
    ).astype(jnp.bfloat16)
    hidden_f = hidden.astype(jnp.float32)
    centred = hidden_f - jnp.mean(hidden_f, axis=-1, keepdims=True)
    inv_std = lax.rsqrt(jnp.mean(centred * centred, axis=-1, keepdims=True) + EPSILON)
    unit_rows = centred * inv_std
    normed = unit_rows.astype(jnp.bfloat16)
    normeds = all_rows(normed)
    qkv_rows = dot_rows(normed, qkv_weight).astype(jnp.bfloat16)

    outgoing = jnp.concatenate([qkv_rows, grad_att], axis=1).reshape(tm_count, half * loc, -1)
    packed = lax.all_to_all(outgoing, "tm", split_axis=0, concat_axis=0, tiled=True)
    result = attention(packed.reshape(rows, 4 * attn_width), loc, attn_width)
    result = lax.all_to_all(
        result.reshape(tm_count, half * loc, 4 * attn_width),
        "tm",
        split_axis=0,
        concat_axis=0,
        tiled=True,
    ).reshape(rows, 4 * attn_width)
    grad_qkv = result[:, : 3 * attn_width]
    attended = result[:, 3 * attn_width :]

    grad_scale = 1.0 / math.sqrt(dp_count * tm_count * rows)

    proj_share = share_of(all_rows(attended), cot_columns)
    qkv_share = share_of(normeds, own_columns(grad_qkv))
    proj_half = halve(proj_share.reshape(high, 2, -1, proj_share.shape[-1]))
    qkv_half = halve(qkv_share.reshape(high, 2, -1, qkv_share.shape[-1]))

    grad_normed = dot_rows_t(grad_qkv, qkv_weight)
    correction = (
        grad_normed
        - jnp.mean(grad_normed, axis=-1, keepdims=True)
        - unit_rows * jnp.mean(grad_normed * unit_rows, axis=-1, keepdims=True)
    )
    grad_hidden = (cotangent_rows.astype(jnp.float32) + inv_std * correction).astype(jnp.bfloat16)
    conv_share = share_of(conv_lefts, own_columns(grad_hidden))
    conv_share = jnp.transpose(
        conv_share.reshape(3, high, 2, -1, conv_share.shape[-1]), (1, 2, 0, 3, 4)
    ).reshape(high, 2, -1, conv_share.shape[-1])
    conv_half = halve(conv_share)
    qkv_sum = join(scatter_high(qkv_half, grad_scale), 1)
    rest_sum = join(
        scatter_high(jnp.concatenate([conv_half, proj_half], axis=1), grad_scale), 1
    )

    grad_four = grad_hidden.reshape(tm_count, half, loc, width)
    rim_after = from_behind(grad_four[:, 0], "tm", -1)
    grad_next = jnp.concatenate([grad_four[:, 1:], rim_after[:, None]], axis=1)
    grad_even = dot_rows_t(grad_hidden, tap_one).astype(jnp.bfloat16)
    grad_odd = (dot_rows_t(grad_hidden, tap_two) + dot_rows_t(as_rows(grad_next), tap_zero)).astype(
        jnp.bfloat16
    )
    by_frame = (tm_count, half, loc, width)
    input_grad = jnp.transpose(
        jnp.stack([grad_even.reshape(by_frame), grad_odd.reshape(by_frame)], axis=0),
        (2, 0, 1, 3, 4),
    ).reshape(latents.shape)

    qkv_grad = join(qkv_sum, 0)
    rest_grad = join(rest_sum, 0)
    size = width // tm_count
    conv_grad = jnp.concatenate(
        [rest_grad[tap * size : (tap + 1) * size] for tap in range(3)], axis=1
    )
    proj_grad = rest_grad[3 * size :]
    return (input_grad, conv_grad, qkv_grad, proj_grad)


def solution(mesh):
    return jax.shard_map(
        local,
        mesh=mesh,
        in_specs=(P("dp", "tm", None, None), P(), P(), P(), P("dp", "tm", None, None)),
        out_specs=(P("dp", "tm", None, None), P("tm", None), P("tm", None), P("tm", None)),
        check_vma=False,
    )
```

```python
import functools
import math

import jax
import jax.numpy as jnp
from jax import lax
from jax.experimental import pallas as pl
from jax.experimental.pallas import tpu as pltpu
from jax.sharding import PartitionSpec as P

HEADS = 10
HEAD = 64


EPSILON = 1e-05


def from_behind(shard, axis, by):
    devices = lax.axis_size(axis)
    pairs = [(i, i + by) for i in range(devices) if 0 <= i + by < devices]
    return lax.ppermute(shard, axis, pairs)


def swap(shard, axis, bit):
    devices = lax.axis_size(axis)
    return lax.ppermute(shard, axis, [(i, i ^ (1 << bit)) for i in range(devices)])


def bit_of(axis, bit):
    return (lax.axis_index(axis) >> bit) & 1


def dot_rows(left_side, right_side):
    return jnp.dot(left_side, right_side, preferred_element_type=jnp.float32)


def dot_rows_t(left_side, right_side):
    return lax.dot_general(
        left_side, right_side, (((1,), (1,)), ((), ())), preferred_element_type=jnp.float32
    )


def dot_columns(left_side, right_side):
    return lax.dot_general(
        left_side, right_side, (((0,), (0,)), ((), ())), preferred_element_type=jnp.float32
    )


def attention_kernel(loc, width, packed_ref, result_ref):
    rows = packed_ref.shape[0]
    row_at = lax.broadcasted_iota(jnp.int32, (rows, rows), 0)
    column_at = lax.broadcasted_iota(jnp.int32, (rows, rows), 1)
    same = (row_at % loc) == (column_at % loc)
    lane = lax.broadcasted_iota(jnp.int32, (rows, 2 * HEAD), 1)
    scale = 1.0 / math.sqrt(HEAD)
    for pair in range(width // (2 * HEAD)):
        first = pair * 2 * HEAD
        q = packed_ref[:, first : first + 2 * HEAD]
        k = packed_ref[:, width + first : width + first + 2 * HEAD]
        v = packed_ref[:, 2 * width + first : 2 * width + first + 2 * HEAD]
        g = packed_ref[:, 3 * width + first : 3 * width + first + 2 * HEAD]
        zero = jnp.zeros_like(q)
        grad_q = grad_k = grad_v = attended = None
        kept = []
        for head in range(2):
            mine = (lane >= HEAD) if head else (lane < HEAD)
            q_h = jnp.where(mine, q, zero)
            v_h = jnp.where(mine, v, zero)
            g_h = jnp.where(mine, g, zero)
            scores = jnp.where(same, dot_rows_t(q_h, k) * scale, -1e30)
            expo = jnp.exp(scores - jnp.max(scores, axis=1, keepdims=True))
            probs = expo * (1.0 / jnp.sum(expo, axis=1, keepdims=True))
            probs_b = probs.astype(jnp.bfloat16)
            part = dot_rows(probs_b, v_h)
            attended = part if attended is None else attended + part
            part = dot_columns(probs_b, g_h)
            grad_v = part if grad_v is None else grad_v + part
            grad_probs = dot_rows_t(g_h, v)
            kept.append((mine, q_h, probs, grad_probs))
        attended_b = attended.astype(jnp.bfloat16)
        product = g.astype(jnp.float32) * attended_b.astype(jnp.float32)
        for mine, q_h, probs, grad_probs in kept:
            k_h = jnp.where(mine, k, zero)
            delta = jnp.sum(jnp.where(mine, product, 0.0), axis=1, keepdims=True)
            grad_scores = (probs * (grad_probs - delta) * scale).astype(jnp.bfloat16)
            part = dot_rows(grad_scores, k_h)
            grad_q = part if grad_q is None else grad_q + part
            part = dot_columns(grad_scores, q_h)
            grad_k = part if grad_k is None else grad_k + part
        result_ref[:, first : first + 2 * HEAD] = grad_q.astype(jnp.bfloat16)
        result_ref[:, width + first : width + first + 2 * HEAD] = grad_k.astype(jnp.bfloat16)
        result_ref[:, 2 * width + first : 2 * width + first + 2 * HEAD] = grad_v.astype(
            jnp.bfloat16
        )
        result_ref[:, 3 * width + first : 3 * width + first + 2 * HEAD] = attended_b


def attention(packed, loc, width):
    rows = packed.shape[0]
    return pl.pallas_call(
        functools.partial(attention_kernel, loc, width),
        out_shape=jax.ShapeDtypeStruct(packed.shape, jnp.bfloat16),
        in_specs=[pl.BlockSpec(memory_space=pltpu.VMEM)],
        out_specs=pl.BlockSpec(memory_space=pltpu.VMEM),
        compiler_params=pltpu.CompilerParams(vmem_limit_bytes=40 * 1024 * 1024),
        cost_estimate=pl.CostEstimate(
            flops=14 * HEADS * rows * rows * 2 * HEAD,
            bytes_accessed=2 * packed.size * 2,
            transcendentals=HEADS * rows * rows,
        ),
    )(packed)


def halve(array, position, axis, bit):
    mine = bit_of(axis, bit)
    away = lax.dynamic_index_in_dim(array, 1 - mine, position, keepdims=False)
    stay = lax.dynamic_index_in_dim(array, mine, position, keepdims=False)
    came = swap(away, axis, bit)
    return (stay.astype(jnp.float32) + came.astype(jnp.float32)).astype(jnp.bfloat16)


def join(array, axis, bit, position):
    came = swap(array, axis, bit)
    first = bit_of(axis, bit) == 0
    return jnp.concatenate(
        [jnp.where(first, array, came), jnp.where(first, came, array)], axis=position
    )


def scatter_low(share, bits, y_first):
    if y_first:
        share = halve(share, bits + 1, "dp", 1)
        share = halve(share, bits, "tm", 0)
    else:
        share = halve(share, bits, "tm", 0)
        share = halve(share, bits, "dp", 1)
    share = jnp.moveaxis(share, 0, bits - 1)
    return share.reshape(share.shape[: bits - 1] + (-1, share.shape[-1]))


def scatter_high(share, bits, scale):
    for bit in range(1, bits):
        share = halve(share, bits - 1 - bit, "tm", bit)
    return (share.astype(jnp.float32) * scale).astype(jnp.bfloat16)


def local(latents, conv_weight, qkv_weight, out_weight, out_cotangent):
    videos, frames, places, width = latents.shape
    half = frames // 2
    attn_width = out_weight.shape[0]
    dp_count = lax.axis_size("dp")
    tm_count = lax.axis_size("tm")
    bits = tm_count.bit_length() - 1
    loc = places // tm_count
    rows = half * places
    core = bit_of("dp", 0)

    def as_rows(values):
        return values.reshape(rows, values.shape[-1])

    def own_half(values, which):
        size = values.shape[-1] // 2
        return lax.dynamic_slice_in_dim(values, which * size, size, axis=values.ndim - 1)

    split = latents.reshape(half, 2, tm_count, loc, width)
    rim_input = from_behind(split[half - 1, 1], "tm", 1)
    split = jnp.transpose(split, (1, 2, 0, 3, 4))
    even_frames, odd_frames = split[0], split[1]
    prev_frames = jnp.concatenate([rim_input[:, None], odd_frames[:, : half - 1]], axis=1)
    cotangent_rows = as_rows(
        jnp.transpose(out_cotangent.reshape(half, tm_count, loc, width), (1, 0, 2, 3))
    )

    tap_zero = conv_weight[:, :width]
    tap_one = conv_weight[:, width : 2 * width]
    tap_two = conv_weight[:, 2 * width :]
    prev_rows = as_rows(prev_frames)
    even_rows = as_rows(even_frames)
    odd_rows = as_rows(odd_frames)
    conv_left = jnp.concatenate([prev_rows, even_rows, odd_rows], axis=1)
    conv_left_other = swap(conv_left, "dp", 0)
    cot_half = own_half(cotangent_rows, core)
    cot_half_other = swap(own_half(cotangent_rows, 1 - core), "dp", 0)

    grad_att = dot_rows_t(cotangent_rows, out_weight).astype(jnp.bfloat16)
    hidden = (
        dot_rows(prev_rows, tap_zero) + dot_rows(even_rows, tap_one) + dot_rows(odd_rows, tap_two)
    ).astype(jnp.bfloat16)
    hidden_f = hidden.astype(jnp.float32)
    centred = hidden_f - jnp.mean(hidden_f, axis=-1, keepdims=True)
    inv_std = lax.rsqrt(jnp.mean(centred * centred, axis=-1, keepdims=True) + EPSILON)
    unit_rows = centred * inv_std
    normed = unit_rows.astype(jnp.bfloat16)
    normed_other = swap(normed, "dp", 0)
    qkv_rows = dot_rows(normed, qkv_weight).astype(jnp.bfloat16)

    outgoing = jnp.concatenate([qkv_rows, grad_att], axis=1).reshape(tm_count, half * loc, -1)
    packed = lax.all_to_all(outgoing, "tm", split_axis=0, concat_axis=0, tiled=True)
    result = attention(packed.reshape(rows, 4 * attn_width), loc, attn_width)
    result = lax.all_to_all(
        result.reshape(tm_count, half * loc, 4 * attn_width),
        "tm",
        split_axis=0,
        concat_axis=0,
        tiled=True,
    ).reshape(rows, 4 * attn_width)
    grad_qkv = result[:, : 3 * attn_width]
    attended = result[:, 3 * attn_width :]

    grad_scale = 1.0 / math.sqrt(dp_count * tm_count * rows)

    def by_bits(share, taps, parts):
        channels = share.shape[0] // taps
        size = channels // tm_count // math.prod(parts)
        return share.reshape((taps,) + (2,) * bits + parts + (size, share.shape[1]))

    def pieces(share, taps):
        share = by_bits(share, taps, (2, 2))
        ahead = lax.index_in_dim(share, 0, bits + 1, keepdims=False)
        behind = lax.index_in_dim(share, 1, bits + 1, keepdims=False)
        return [scatter_low(ahead, bits, False), scatter_low(behind, bits, True)]

    attended_other = swap(attended, "dp", 0)
    proj_share = (
        dot_columns(attended, cot_half) + dot_columns(attended_other, cot_half_other)
    ).astype(jnp.bfloat16)
    gq_half = own_half(grad_qkv, core)
    gq_half_other = swap(own_half(grad_qkv, 1 - core), "dp", 0)
    qkv_share = (dot_columns(normed, gq_half) + dot_columns(normed_other, gq_half_other)).astype(
        jnp.bfloat16
    )

    grad_normed = dot_rows_t(grad_qkv, qkv_weight)
    correction = (
        grad_normed
        - jnp.mean(grad_normed, axis=-1, keepdims=True)
        - unit_rows * jnp.mean(grad_normed * unit_rows, axis=-1, keepdims=True)
    )
    grad_hidden = (cotangent_rows.astype(jnp.float32) + inv_std * correction).astype(jnp.bfloat16)
    gh_half = own_half(grad_hidden, core)
    gh_half_other = swap(own_half(grad_hidden, 1 - core), "dp", 0)
    conv_share = (
        dot_columns(conv_left, gh_half) + dot_columns(conv_left_other, gh_half_other)
    ).astype(jnp.bfloat16)

    proj_pieces = [scatter_low(by_bits(proj_share, 1, (2,)), bits, True)]
    qkv_pieces = pieces(qkv_share, 1)
    conv_pieces = pieces(conv_share, 3)
    qkv_sum = scatter_high(jnp.concatenate(qkv_pieces, axis=bits - 1), bits, grad_scale)
    rest_sum = scatter_high(
        jnp.concatenate(conv_pieces + proj_pieces, axis=bits - 1), bits, grad_scale
    )
    qkv_both = join(join(qkv_sum[None], "dp", 1, 0), "dp", 0, 2)
    rest_both = join(join(rest_sum[None], "dp", 1, 0), "dp", 0, 2)

    grad_hidden, _ = lax.optimization_barrier((grad_hidden, conv_share))
    grad_four = grad_hidden.reshape(tm_count, half, loc, width)
    rim_after = from_behind(grad_four[:, 0], "tm", -1)
    grad_next = jnp.concatenate([grad_four[:, 1:], rim_after[:, None]], axis=1)
    grad_even = dot_rows_t(grad_hidden, tap_one).astype(jnp.bfloat16)
    grad_odd = (dot_rows_t(grad_hidden, tap_two) + dot_rows_t(as_rows(grad_next), tap_zero)).astype(
        jnp.bfloat16
    )
    by_frame = (tm_count, half, loc, width)
    input_grad = jnp.transpose(
        jnp.stack([grad_even.reshape(by_frame), grad_odd.reshape(by_frame)], axis=0),
        (2, 0, 1, 3, 4),
    ).reshape(latents.shape)

    size = width // tm_count // 4
    qkv_grad = jnp.transpose(qkv_both.reshape(2, 2, size, -1), (1, 0, 2, 3)).reshape(4 * size, -1)
    conv_both = rest_both[:, : 6 * size].reshape(2, 2, 3, size, width)
    conv_grad = jnp.transpose(conv_both, (1, 0, 3, 2, 4)).reshape(4 * size, 3 * width)
    proj_grad = rest_both[:, 6 * size :].reshape(-1, width)
    return (input_grad, conv_grad, qkv_grad, proj_grad)


def solution(mesh):
    return jax.shard_map(
        local,
        mesh=mesh,
        in_specs=(P("dp", "tm", None, None), P(), P(), P(), P("dp", "tm", None, None)),
        out_specs=(P("dp", "tm", None, None), P("tm", None), P("tm", None), P("tm", None)),
        check_vma=False,
    )
```

```python
import functools
import math

import jax
import jax.numpy as jnp
from jax import lax
from jax.experimental import pallas as pl
from jax.experimental.pallas import tpu as pltpu
from jax.sharding import PartitionSpec as P

HEADS = 10
HEAD = 64


EPSILON = 1e-05


def from_behind(shard, axis, by):
    devices = lax.axis_size(axis)
    pairs = [(i, i + by) for i in range(devices) if 0 <= i + by < devices]
    return lax.ppermute(shard, axis, pairs)


def swap(shard, axis, bit):
    devices = lax.axis_size(axis)
    return lax.ppermute(shard, axis, [(i, i ^ (1 << bit)) for i in range(devices)])


def bit_of(axis, bit):
    return (lax.axis_index(axis) >> bit) & 1


def dot_rows(left_side, right_side):
    return jnp.dot(left_side, right_side, preferred_element_type=jnp.float32)


def dot_rows_t(left_side, right_side):
    return lax.dot_general(
        left_side, right_side, (((1,), (1,)), ((), ())), preferred_element_type=jnp.float32
    )


def dot_columns(left_side, right_side):
    return lax.dot_general(
        left_side, right_side, (((0,), (0,)), ((), ())), preferred_element_type=jnp.float32
    )


def attention_kernel(loc, width, packed_ref, result_ref):
    rows = packed_ref.shape[0]
    row_at = lax.broadcasted_iota(jnp.int32, (rows, rows), 0)
    column_at = lax.broadcasted_iota(jnp.int32, (rows, rows), 1)
    same = (row_at % loc) == (column_at % loc)
    lane = lax.broadcasted_iota(jnp.int32, (rows, 2 * HEAD), 1)
    scale = 1.0 / math.sqrt(HEAD)
    for pair in range(width // (2 * HEAD)):
        first = pair * 2 * HEAD
        q = packed_ref[:, first : first + 2 * HEAD]
        k = packed_ref[:, width + first : width + first + 2 * HEAD]
        v = packed_ref[:, 2 * width + first : 2 * width + first + 2 * HEAD]
        g = packed_ref[:, 3 * width + first : 3 * width + first + 2 * HEAD]
        zero = jnp.zeros_like(q)
        grad_q = grad_k = grad_v = attended = None
        kept = []
        for head in range(2):
            mine = (lane >= HEAD) if head else (lane < HEAD)
            q_h = jnp.where(mine, q, zero)
            v_h = jnp.where(mine, v, zero)
            g_h = jnp.where(mine, g, zero)
            scores = jnp.where(same, dot_rows_t(q_h, k) * scale, -1e30)
            expo = jnp.exp(scores - jnp.max(scores, axis=1, keepdims=True))
            probs = expo * (1.0 / jnp.sum(expo, axis=1, keepdims=True))
            probs_b = probs.astype(jnp.bfloat16)
            part = dot_rows(probs_b, v_h)
            attended = part if attended is None else attended + part
            part = dot_columns(probs_b, g_h)
            grad_v = part if grad_v is None else grad_v + part
            grad_probs = dot_rows_t(g_h, v)
            kept.append((mine, q_h, probs, grad_probs))
        attended_b = attended.astype(jnp.bfloat16)
        product = g.astype(jnp.float32) * attended_b.astype(jnp.float32)
        for mine, q_h, probs, grad_probs in kept:
            k_h = jnp.where(mine, k, zero)
            delta = jnp.sum(jnp.where(mine, product, 0.0), axis=1, keepdims=True)
            grad_scores = (probs * (grad_probs - delta) * scale).astype(jnp.bfloat16)
            part = dot_rows(grad_scores, k_h)
            grad_q = part if grad_q is None else grad_q + part
            part = dot_columns(grad_scores, q_h)
            grad_k = part if grad_k is None else grad_k + part
        result_ref[:, first : first + 2 * HEAD] = grad_q.astype(jnp.bfloat16)
        result_ref[:, width + first : width + first + 2 * HEAD] = grad_k.astype(jnp.bfloat16)
        result_ref[:, 2 * width + first : 2 * width + first + 2 * HEAD] = grad_v.astype(
            jnp.bfloat16
        )
        result_ref[:, 3 * width + first : 3 * width + first + 2 * HEAD] = attended_b


def attention(packed, loc, width):
    rows = packed.shape[0]
    return pl.pallas_call(
        functools.partial(attention_kernel, loc, width),
        out_shape=jax.ShapeDtypeStruct(packed.shape, jnp.bfloat16),
        in_specs=[pl.BlockSpec(memory_space=pltpu.VMEM)],
        out_specs=pl.BlockSpec(memory_space=pltpu.VMEM),
        compiler_params=pltpu.CompilerParams(vmem_limit_bytes=40 * 1024 * 1024),
        cost_estimate=pl.CostEstimate(
            flops=14 * HEADS * rows * rows * 2 * HEAD,
            bytes_accessed=2 * packed.size * 2,
            transcendentals=HEADS * rows * rows,
        ),
    )(packed)


def sum_kernel(scale, high, *refs):
    ins, outs = refs[:3], refs[3:6]
    scratch = [refs[6 + 6 * i : 12 + 6 * i] for i in range(3)]
    send_sem, recv_sem = refs[24], refs[25]
    dp, tm = lax.axis_index("dp"), lax.axis_index("tm")
    core, my = dp % 2, dp // 2
    mx, mz = tm % 2, tm // 2
    x_peer = (dp, tm + 1 - 2 * mx)
    y_peer = (dp + 2 - 4 * my, tm)
    core_peer = (dp + 1 - 2 * core, tm)
    z_peers = [(dp, (mz + d) % high * 2 + mx) for d in range(1, high)]

    barrier = pltpu.get_barrier_semaphore()
    for peer in [x_peer, y_peer, core_peer] + z_peers:
        pl.semaphore_signal(
            barrier, inc=1, device_id=peer, device_id_type=pl.DeviceIdType.MESH
        )
    pl.semaphore_wait(barrier, 3 + len(z_peers))

    wide = ins[0].shape[-1]
    cut = wide // 256 * 128 if wide > 256 else wide
    low, rest = pl.ds(0, cut), pl.ds(cut, wide - cut)
    full = slice(None)
    units = [
        (0, 0, True, low), (0, 1, False, low),
        (0, 0, True, rest), (0, 1, False, rest),
        (0, 2, True, low), (1, 0, False, full),
        (0, 2, True, rest), (2, 0, False, full),
    ]

    def copy(unit, kind, source, target, peer):
        return pltpu.make_async_remote_copy(
            src_ref=source,
            dst_ref=target,
            send_sem=send_sem.at[unit, kind],
            recv_sem=recv_sem.at[unit, kind],
            device_id=peer,
            device_id_type=pl.DeviceIdType.MESH,
        )

    def first(unit):
        tensor, tap, x_first, cols = units[unit]
        share, r1 = ins[tensor], scratch[tensor][0]
        if x_first:
            source, peer = share.at[tap, :, 1 - mx, :, :, cols], x_peer
        else:
            source, peer = share.at[tap, :, :, 1 - my, :, cols], y_peer
        return [copy(unit, 0, source, r1.at[tap, :, :, :, cols], peer)]

    def second(unit):
        tensor, tap, x_first, cols = units[unit]
        s1, r2 = scratch[tensor][1], scratch[tensor][2]
        away, peer = (1 - my, y_peer) if x_first else (1 - mx, x_peer)
        return [copy(unit, 1, s1.at[tap, :, away, :, cols], r2.at[tap, :, :, cols], peer)]

    def third(unit):
        tensor, tap, x_first, cols = units[unit]
        s2, r3 = scratch[tensor][3], scratch[tensor][4]
        return [
            copy(
                unit,
                1 + d,
                s2.at[tap, (mz + d) % high, :, cols],
                r3.at[d - 1, tap, :, cols],
                z_peers[d - 1],
            )
            for d in range(1, high)
        ]

    def fourth(unit):
        tensor, tap, x_first, cols = units[unit]
        place = scratch[tensor][5].at[core, tap, my, :, cols]
        return [copy(unit, 1 + high, place, place, y_peer)]

    def fifth(unit):
        tensor, tap, x_first, cols = units[unit]
        place = scratch[tensor][5].at[core, tap, :, :, cols]
        return [copy(unit, 2 + high, place, place, core_peer)]

    def add_first(unit):
        tensor, tap, x_first, cols = units[unit]
        share, r1, s1 = ins[tensor], scratch[tensor][0], scratch[tensor][1]
        stay = share[tap, :, mx, :, :, cols] if x_first else share[tap, :, :, my, :, cols]
        came = r1[tap, :, :, :, cols]
        s1[tap, :, :, :, cols] = (stay.astype(jnp.float32) + came.astype(jnp.float32)).astype(
            jnp.bfloat16
        )

    def add_second(unit):
        tensor, tap, x_first, cols = units[unit]
        s1, r2, s2 = scratch[tensor][1:4]
        stay = s1[tap, :, my if x_first else mx, :, cols]
        came = r2[tap, :, :, cols]
        s2[tap, :, :, cols] = (stay.astype(jnp.float32) + came.astype(jnp.float32)).astype(
            jnp.bfloat16
        )

    def add_third(unit):
        tensor, tap, x_first, cols = units[unit]
        s2, r3, gathered = scratch[tensor][3:6]
        total = s2[tap, mz, :, cols].astype(jnp.float32)
        for d in range(1, high):
            total += r3[d - 1, tap, :, cols].astype(jnp.float32)
        gathered[core, tap, my, :, cols] = (total * scale).astype(jnp.bfloat16)

    stages = [first, second, third, fourth, fifth]
    adds = [add_first, add_second, add_third, None]
    steps = len(units) // 2
    flights = {}

    def start(stage, step):
        for unit in (2 * step, 2 * step + 1):
            flights[stage, unit] = stages[stage](unit)
            for flight in flights[stage, unit]:
                flight.start()

    def advance(stage, step):
        for unit in (2 * step, 2 * step + 1):
            for flight in flights[stage, unit]:
                flight.wait()
            if stage < 4:
                if adds[stage] is not None:
                    adds[stage](unit)
                flights[stage + 1, unit] = stages[stage + 1](unit)
                for flight in flights[stage + 1, unit]:
                    flight.start()

    start(0, 0)
    start(0, 1)
    for time in range(steps + 4):
        for stage in range(5):
            step = time - stage
            if 0 <= step < steps:
                advance(stage, step)
                if stage == 0 and step + 2 < steps:
                    start(0, step + 2)
    for tensor in range(3):
        outs[tensor][...] = scratch[tensor][5][...]


def sum_over_devices(shares, scale):
    high = shares[0].shape[1]
    scratch = []
    out_shapes = []
    for share in shares:
        taps, _, _, _, rows, columns = share.shape
        for shape in (
            (taps, high, 2, rows, columns),
            (taps, high, 2, rows, columns),
            (taps, high, rows, columns),
            (taps, high, rows, columns),
            (high - 1, taps, rows, columns),
            (2, taps, 2, rows, columns),
        ):
            scratch.append(pltpu.VMEM(shape, jnp.bfloat16))
        out_shapes.append(jax.ShapeDtypeStruct((2, taps, 2, rows, columns), jnp.bfloat16))
    semaphores = pltpu.SemaphoreType.DMA((8, high + 3))
    size = sum(share.size for share in shares)
    return pl.pallas_call(
        functools.partial(sum_kernel, scale, high),
        out_shape=out_shapes,
        in_specs=[pl.BlockSpec(memory_space=pltpu.VMEM)] * 3,
        out_specs=[pl.BlockSpec(memory_space=pltpu.VMEM)] * 3,
        scratch_shapes=scratch + [semaphores, semaphores],
        compiler_params=pltpu.CompilerParams(
            collective_id=0, has_side_effects=True, vmem_limit_bytes=50 * 1024 * 1024
        ),
        cost_estimate=pl.CostEstimate(
            flops=size, bytes_accessed=20 * size, transcendentals=0
        ),
    )(*shares)


def local(latents, conv_weight, qkv_weight, out_weight, out_cotangent):
    videos, frames, places, width = latents.shape
    half = frames // 2
    attn_width = out_weight.shape[0]
    dp_count = lax.axis_size("dp")
    tm_count = lax.axis_size("tm")
    loc = places // tm_count
    rows = half * places
    core = bit_of("dp", 0)

    def as_rows(values):
        return values.reshape(rows, values.shape[-1])

    def own_half(values, which):
        size = values.shape[-1] // 2
        return lax.dynamic_slice_in_dim(values, which * size, size, axis=values.ndim - 1)

    split = latents.reshape(half, 2, tm_count, loc, width)
    rim_input = from_behind(split[half - 1, 1], "tm", 1)
    split = jnp.transpose(split, (1, 2, 0, 3, 4))
    even_frames, odd_frames = split[0], split[1]
    prev_frames = jnp.concatenate([rim_input[:, None], odd_frames[:, : half - 1]], axis=1)
    cotangent_rows = as_rows(
        jnp.transpose(out_cotangent.reshape(half, tm_count, loc, width), (1, 0, 2, 3))
    )

    tap_zero = conv_weight[:, :width]
    tap_one = conv_weight[:, width : 2 * width]
    tap_two = conv_weight[:, 2 * width :]
    prev_rows = as_rows(prev_frames)
    even_rows = as_rows(even_frames)
    odd_rows = as_rows(odd_frames)
    conv_left = jnp.concatenate([prev_rows, even_rows, odd_rows], axis=1)
    conv_left_other = swap(conv_left, "dp", 0)
    cot_half = own_half(cotangent_rows, core)
    cot_half_other = swap(own_half(cotangent_rows, 1 - core), "dp", 0)

    grad_att = dot_rows_t(cotangent_rows, out_weight).astype(jnp.bfloat16)
    hidden = (
        dot_rows(prev_rows, tap_zero) + dot_rows(even_rows, tap_one) + dot_rows(odd_rows, tap_two)
    ).astype(jnp.bfloat16)
    hidden_f = hidden.astype(jnp.float32)
    centred = hidden_f - jnp.mean(hidden_f, axis=-1, keepdims=True)
    inv_std = lax.rsqrt(jnp.mean(centred * centred, axis=-1, keepdims=True) + EPSILON)
    unit_rows = centred * inv_std
    normed = unit_rows.astype(jnp.bfloat16)
    normed_other = swap(normed, "dp", 0)
    qkv_rows = dot_rows(normed, qkv_weight).astype(jnp.bfloat16)

    outgoing = jnp.concatenate([qkv_rows, grad_att], axis=1).reshape(tm_count, half * loc, -1)
    packed = lax.all_to_all(outgoing, "tm", split_axis=0, concat_axis=0, tiled=True)
    result = attention(packed.reshape(rows, 4 * attn_width), loc, attn_width)
    result = lax.all_to_all(
        result.reshape(tm_count, half * loc, 4 * attn_width),
        "tm",
        split_axis=0,
        concat_axis=0,
        tiled=True,
    ).reshape(rows, 4 * attn_width)
    grad_qkv = result[:, : 3 * attn_width]
    attended = result[:, 3 * attn_width :]

    grad_scale = 1.0 / math.sqrt(dp_count * tm_count * rows)

    def by_owner(share, taps):
        return share.reshape(taps, tm_count // 2, 2, 2, -1, share.shape[1])

    attended_other = swap(attended, "dp", 0)
    proj_share = (
        dot_columns(attended, cot_half) + dot_columns(attended_other, cot_half_other)
    ).astype(jnp.bfloat16)
    gq_half = own_half(grad_qkv, core)
    gq_half_other = swap(own_half(grad_qkv, 1 - core), "dp", 0)
    qkv_share = (dot_columns(normed, gq_half) + dot_columns(normed_other, gq_half_other)).astype(
        jnp.bfloat16
    )

    grad_normed = dot_rows_t(grad_qkv, qkv_weight)
    correction = (
        grad_normed
        - jnp.mean(grad_normed, axis=-1, keepdims=True)
        - unit_rows * jnp.mean(grad_normed * unit_rows, axis=-1, keepdims=True)
    )
    grad_hidden = (cotangent_rows.astype(jnp.float32) + inv_std * correction).astype(jnp.bfloat16)
    gh_half = own_half(grad_hidden, core)
    gh_half_other = swap(own_half(grad_hidden, 1 - core), "dp", 0)
    conv_share = (
        dot_columns(conv_left, gh_half) + dot_columns(conv_left_other, gh_half_other)
    ).astype(jnp.bfloat16)

    conv_sum, qkv_sum, proj_sum = sum_over_devices(
        [by_owner(conv_share, 3), by_owner(qkv_share, 1), by_owner(proj_share, 1)], grad_scale
    )

    grad_four = grad_hidden.reshape(tm_count, half, loc, width)
    rim_after = from_behind(grad_four[:, 0], "tm", -1)
    grad_next = jnp.concatenate([grad_four[:, 1:], rim_after[:, None]], axis=1)
    grad_even = dot_rows_t(grad_hidden, tap_one).astype(jnp.bfloat16)
    grad_odd = (dot_rows_t(grad_hidden, tap_two) + dot_rows_t(as_rows(grad_next), tap_zero)).astype(
        jnp.bfloat16
    )
    by_frame = (tm_count, half, loc, width)
    input_grad = jnp.transpose(
        jnp.stack([grad_even.reshape(by_frame), grad_odd.reshape(by_frame)], axis=0),
        (2, 0, 1, 3, 4),
    ).reshape(latents.shape)

    def assembled(gathered):
        ordered = jnp.transpose(gathered, (2, 3, 1, 0, 4))
        return ordered.reshape(ordered.shape[0] * ordered.shape[1], -1)

    conv_grad = assembled(conv_sum)
    qkv_grad = assembled(qkv_sum)
    proj_grad = assembled(proj_sum)
    return (input_grad, conv_grad, qkv_grad, proj_grad)


def solution(mesh):
    return jax.shard_map(
        local,
        mesh=mesh,
        in_specs=(P("dp", "tm", None, None), P(), P(), P(), P("dp", "tm", None, None)),
        out_specs=(P("dp", "tm", None, None), P("tm", None), P("tm", None), P("tm", None)),
        check_vma=False,
    )
```

```python
import functools
import math

import jax
import jax.numpy as jnp
from jax import lax
from jax.experimental import pallas as pl
from jax.experimental.pallas import tpu as pltpu
from jax.sharding import PartitionSpec as P

HEADS = 10
HEAD = 64


EPSILON = 1e-05


def from_behind(shard, axis, by):
    devices = lax.axis_size(axis)
    pairs = [(i, i + by) for i in range(devices) if 0 <= i + by < devices]
    return lax.ppermute(shard, axis, pairs)


def swap(shard, axis, bit):
    devices = lax.axis_size(axis)
    return lax.ppermute(shard, axis, [(i, i ^ (1 << bit)) for i in range(devices)])


def bit_of(axis, bit):
    return (lax.axis_index(axis) >> bit) & 1


def dot_rows(left_side, right_side):
    return jnp.dot(left_side, right_side, preferred_element_type=jnp.float32)


def dot_rows_t(left_side, right_side):
    return lax.dot_general(
        left_side, right_side, (((1,), (1,)), ((), ())), preferred_element_type=jnp.float32
    )


def dot_columns(left_side, right_side):
    return lax.dot_general(
        left_side, right_side, (((0,), (0,)), ((), ())), preferred_element_type=jnp.float32
    )


def attention_kernel(loc, width, packed_ref, result_ref):
    rows = packed_ref.shape[0]
    row_at = lax.broadcasted_iota(jnp.int32, (rows, rows), 0)
    column_at = lax.broadcasted_iota(jnp.int32, (rows, rows), 1)
    same = (row_at % loc) == (column_at % loc)
    lane = lax.broadcasted_iota(jnp.int32, (rows, 2 * HEAD), 1)
    scale = 1.0 / math.sqrt(HEAD)
    for pair in range(width // (2 * HEAD)):
        first = pair * 2 * HEAD
        q = packed_ref[:, first : first + 2 * HEAD]
        k = packed_ref[:, width + first : width + first + 2 * HEAD]
        v = packed_ref[:, 2 * width + first : 2 * width + first + 2 * HEAD]
        g = packed_ref[:, 3 * width + first : 3 * width + first + 2 * HEAD]
        zero = jnp.zeros_like(q)
        grad_q = grad_k = grad_v = attended = None
        kept = []
        for head in range(2):
            mine = (lane >= HEAD) if head else (lane < HEAD)
            q_h = jnp.where(mine, q, zero)
            v_h = jnp.where(mine, v, zero)
            g_h = jnp.where(mine, g, zero)
            scores = jnp.where(same, dot_rows_t(q_h, k) * scale, -1e30)
            expo = jnp.exp(scores - jnp.max(scores, axis=1, keepdims=True))
            probs = expo * (1.0 / jnp.sum(expo, axis=1, keepdims=True))
            probs_b = probs.astype(jnp.bfloat16)
            part = dot_rows(probs_b, v_h)
            attended = part if attended is None else attended + part
            part = dot_columns(probs_b, g_h)
            grad_v = part if grad_v is None else grad_v + part
            grad_probs = dot_rows_t(g_h, v)
            kept.append((mine, q_h, probs, grad_probs))
        attended_b = attended.astype(jnp.bfloat16)
        product = g.astype(jnp.float32) * attended_b.astype(jnp.float32)
        for mine, q_h, probs, grad_probs in kept:
            k_h = jnp.where(mine, k, zero)
            delta = jnp.sum(jnp.where(mine, product, 0.0), axis=1, keepdims=True)
            grad_scores = (probs * (grad_probs - delta) * scale).astype(jnp.bfloat16)
            part = dot_rows(grad_scores, k_h)
            grad_q = part if grad_q is None else grad_q + part
            part = dot_columns(grad_scores, q_h)
            grad_k = part if grad_k is None else grad_k + part
        result_ref[:, first : first + 2 * HEAD] = grad_q.astype(jnp.bfloat16)
        result_ref[:, width + first : width + first + 2 * HEAD] = grad_k.astype(jnp.bfloat16)
        result_ref[:, 2 * width + first : 2 * width + first + 2 * HEAD] = grad_v.astype(
            jnp.bfloat16
        )
        result_ref[:, 3 * width + first : 3 * width + first + 2 * HEAD] = attended_b


def attention(packed, loc, width):
    rows = packed.shape[0]
    return pl.pallas_call(
        functools.partial(attention_kernel, loc, width),
        out_shape=jax.ShapeDtypeStruct(packed.shape, jnp.bfloat16),
        in_specs=[pl.BlockSpec(memory_space=pltpu.VMEM)],
        out_specs=pl.BlockSpec(memory_space=pltpu.VMEM),
        compiler_params=pltpu.CompilerParams(vmem_limit_bytes=40 * 1024 * 1024),
        cost_estimate=pl.CostEstimate(
            flops=14 * HEADS * rows * rows * 2 * HEAD,
            bytes_accessed=2 * packed.size * 2,
            transcendentals=HEADS * rows * rows,
        ),
    )(packed)


def sum_kernel(scale, high, *refs):
    ins, outs = refs[:3], refs[3:6]
    scratch = [refs[6 + 6 * i : 12 + 6 * i] for i in range(3)]
    send_sem, recv_sem = refs[24], refs[25]
    dp, tm = lax.axis_index("dp"), lax.axis_index("tm")
    core, my = dp % 2, dp // 2
    mx, mz = tm % 2, tm // 2
    x_peer = (dp, tm + 1 - 2 * mx)
    y_peer = (dp + 2 - 4 * my, tm)
    core_peer = (dp + 1 - 2 * core, tm)
    z_peers = [(dp, (mz + d) % high * 2 + mx) for d in range(1, high)]

    barrier = pltpu.get_barrier_semaphore()
    for peer in [x_peer, y_peer, core_peer] + z_peers:
        pl.semaphore_signal(
            barrier, inc=1, device_id=peer, device_id_type=pl.DeviceIdType.MESH
        )
    pl.semaphore_wait(barrier, 3 + len(z_peers))

    wide = ins[0].shape[-1]
    cut = wide // 256 * 128 if wide > 256 else wide
    low, rest = pl.ds(0, cut), pl.ds(cut, wide - cut)
    full = slice(None)
    units = [
        (0, 0, False, low), (0, 1, True, low),
        (0, 0, False, rest), (1, 0, True, full),
        (0, 2, False, rest), (0, 1, True, rest),
        (0, 2, False, low), (2, 0, True, full),
    ]

    def copy(unit, kind, source, target, peer):
        return pltpu.make_async_remote_copy(
            src_ref=source,
            dst_ref=target,
            send_sem=send_sem.at[unit, kind],
            recv_sem=recv_sem.at[unit, kind],
            device_id=peer,
            device_id_type=pl.DeviceIdType.MESH,
        )

    def first(unit):
        tensor, tap, x_first, cols = units[unit]
        share, r1 = ins[tensor], scratch[tensor][0]
        if x_first:
            source, peer = share.at[tap, :, 1 - mx, :, :, cols], x_peer
        else:
            source, peer = share.at[tap, :, :, 1 - my, :, cols], y_peer
        return [copy(unit, 0, source, r1.at[tap, :, :, :, cols], peer)]

    def second(unit):
        tensor, tap, x_first, cols = units[unit]
        s1, r2 = scratch[tensor][1], scratch[tensor][2]
        away, peer = (1 - my, y_peer) if x_first else (1 - mx, x_peer)
        return [copy(unit, 1, s1.at[tap, :, away, :, cols], r2.at[tap, :, :, cols], peer)]

    def third(unit):
        tensor, tap, x_first, cols = units[unit]
        s2, r3 = scratch[tensor][3], scratch[tensor][4]
        return [
            copy(
                unit,
                1 + d,
                s2.at[tap, (mz + d) % high, :, cols],
                r3.at[d - 1, tap, :, cols],
                z_peers[d - 1],
            )
            for d in range(1, high)
        ]

    def fourth(unit):
        tensor, tap, x_first, cols = units[unit]
        place = scratch[tensor][5].at[core, tap, my, :, cols]
        return [copy(unit, 1 + high, place, place, y_peer)]

    def fifth(unit):
        tensor, tap, x_first, cols = units[unit]
        place = scratch[tensor][5].at[core, tap, :, :, cols]
        return [copy(unit, 2 + high, place, place, core_peer)]

    def add_first(unit):
        tensor, tap, x_first, cols = units[unit]
        share, r1, s1 = ins[tensor], scratch[tensor][0], scratch[tensor][1]
        stay = share[tap, :, mx, :, :, cols] if x_first else share[tap, :, :, my, :, cols]
        came = r1[tap, :, :, :, cols]
        s1[tap, :, :, :, cols] = (stay.astype(jnp.float32) + came.astype(jnp.float32)).astype(
            jnp.bfloat16
        )

    def add_second(unit):
        tensor, tap, x_first, cols = units[unit]
        s1, r2, s2 = scratch[tensor][1:4]
        stay = s1[tap, :, my if x_first else mx, :, cols]
        came = r2[tap, :, :, cols]
        s2[tap, :, :, cols] = (stay.astype(jnp.float32) + came.astype(jnp.float32)).astype(
            jnp.bfloat16
        )

    def add_third(unit):
        tensor, tap, x_first, cols = units[unit]
        s2, r3, gathered = scratch[tensor][3:6]
        total = s2[tap, mz, :, cols].astype(jnp.float32)
        for d in range(1, high):
            total += r3[d - 1, tap, :, cols].astype(jnp.float32)
        gathered[core, tap, my, :, cols] = (total * scale).astype(jnp.bfloat16)

    stages = [first, second, third, fourth, fifth]
    adds = [add_first, add_second, add_third, None]
    steps = len(units) // 2
    flights = {}

    def start(stage, step):
        for unit in (2 * step, 2 * step + 1):
            flights[stage, unit] = stages[stage](unit)
            for flight in flights[stage, unit]:
                flight.start()

    def advance(stage, step):
        for unit in (2 * step, 2 * step + 1):
            for flight in flights[stage, unit]:
                flight.wait()
            if stage < 4:
                if adds[stage] is not None:
                    adds[stage](unit)
                flights[stage + 1, unit] = stages[stage + 1](unit)
                for flight in flights[stage + 1, unit]:
                    flight.start()

    start(0, 0)
    start(0, 1)
    for time in range(steps + 4):
        for stage in range(5):
            step = time - stage
            if 0 <= step < steps:
                advance(stage, step)
                if stage == 0 and step + 2 < steps:
                    start(0, step + 2)
    for tensor in range(3):
        outs[tensor][...] = scratch[tensor][5][...]


def sum_over_devices(shares, scale):
    high = shares[0].shape[1]
    scratch = []
    out_shapes = []
    for share in shares:
        taps, _, _, _, rows, columns = share.shape
        for shape in (
            (taps, high, 2, rows, columns),
            (taps, high, 2, rows, columns),
            (taps, high, rows, columns),
            (taps, high, rows, columns),
            (high - 1, taps, rows, columns),
            (2, taps, 2, rows, columns),
        ):
            scratch.append(pltpu.VMEM(shape, jnp.bfloat16))
        out_shapes.append(jax.ShapeDtypeStruct((2, taps, 2, rows, columns), jnp.bfloat16))
    semaphores = pltpu.SemaphoreType.DMA((8, high + 3))
    size = sum(share.size for share in shares)
    return pl.pallas_call(
        functools.partial(sum_kernel, scale, high),
        out_shape=out_shapes,
        in_specs=[pl.BlockSpec(memory_space=pltpu.VMEM)] * 3,
        out_specs=[pl.BlockSpec(memory_space=pltpu.VMEM)] * 3,
        scratch_shapes=scratch + [semaphores, semaphores],
        compiler_params=pltpu.CompilerParams(
            collective_id=0, has_side_effects=True, vmem_limit_bytes=50 * 1024 * 1024
        ),
        cost_estimate=pl.CostEstimate(
            flops=size, bytes_accessed=20 * size, transcendentals=0
        ),
    )(*shares)


def local(latents, conv_weight, qkv_weight, out_weight, out_cotangent):
    videos, frames, places, width = latents.shape
    half = frames // 2
    attn_width = out_weight.shape[0]
    dp_count = lax.axis_size("dp")
    tm_count = lax.axis_size("tm")
    loc = places // tm_count
    rows = half * places
    core = bit_of("dp", 0)

    def as_rows(values):
        return values.reshape(rows, values.shape[-1])

    def own_half(values, which):
        size = values.shape[-1] // 2
        return lax.dynamic_slice_in_dim(values, which * size, size, axis=values.ndim - 1)

    split = latents.reshape(half, 2, tm_count, loc, width)
    rim_input = from_behind(split[half - 1, 1], "tm", 1)
    split = jnp.transpose(split, (1, 2, 0, 3, 4))
    even_frames, odd_frames = split[0], split[1]
    prev_frames = jnp.concatenate([rim_input[:, None], odd_frames[:, : half - 1]], axis=1)
    cotangent_rows = as_rows(
        jnp.transpose(out_cotangent.reshape(half, tm_count, loc, width), (1, 0, 2, 3))
    )

    tap_zero = conv_weight[:, :width]
    tap_one = conv_weight[:, width : 2 * width]
    tap_two = conv_weight[:, 2 * width :]
    prev_rows = as_rows(prev_frames)
    even_rows = as_rows(even_frames)
    odd_rows = as_rows(odd_frames)
    conv_left = jnp.concatenate([prev_rows, even_rows, odd_rows], axis=1)
    conv_left_other = swap(conv_left, "dp", 0)
    cot_half = own_half(cotangent_rows, core)
    cot_half_other = swap(own_half(cotangent_rows, 1 - core), "dp", 0)

    grad_att = dot_rows_t(cotangent_rows, out_weight).astype(jnp.bfloat16)
    hidden = (
        dot_rows(prev_rows, tap_zero) + dot_rows(even_rows, tap_one) + dot_rows(odd_rows, tap_two)
    ).astype(jnp.bfloat16)
    hidden_f = hidden.astype(jnp.float32)
    centred = hidden_f - jnp.mean(hidden_f, axis=-1, keepdims=True)
    inv_std = lax.rsqrt(jnp.mean(centred * centred, axis=-1, keepdims=True) + EPSILON)
    unit_rows = centred * inv_std
    normed = unit_rows.astype(jnp.bfloat16)
    normed_other = swap(normed, "dp", 0)
    qkv_rows = dot_rows(normed, qkv_weight).astype(jnp.bfloat16)

    outgoing = jnp.concatenate([qkv_rows, grad_att], axis=1).reshape(tm_count, half * loc, -1)
    packed = lax.all_to_all(outgoing, "tm", split_axis=0, concat_axis=0, tiled=True)
    result = attention(packed.reshape(rows, 4 * attn_width), loc, attn_width)
    result = lax.all_to_all(
        result.reshape(tm_count, half * loc, 4 * attn_width),
        "tm",
        split_axis=0,
        concat_axis=0,
        tiled=True,
    ).reshape(rows, 4 * attn_width)
    grad_qkv = result[:, : 3 * attn_width]
    attended = result[:, 3 * attn_width :]

    grad_scale = 1.0 / math.sqrt(dp_count * tm_count * rows)

    def by_owner(share, taps):
        return share.reshape(taps, tm_count // 2, 2, 2, -1, share.shape[1])

    attended_other = swap(attended, "dp", 0)
    proj_share = (
        dot_columns(attended, cot_half) + dot_columns(attended_other, cot_half_other)
    ).astype(jnp.bfloat16)
    gq_half = own_half(grad_qkv, core)
    gq_half_other = swap(own_half(grad_qkv, 1 - core), "dp", 0)
    qkv_share = (dot_columns(normed, gq_half) + dot_columns(normed_other, gq_half_other)).astype(
        jnp.bfloat16
    )

    grad_normed = dot_rows_t(grad_qkv, qkv_weight)
    correction = (
        grad_normed
        - jnp.mean(grad_normed, axis=-1, keepdims=True)
        - unit_rows * jnp.mean(grad_normed * unit_rows, axis=-1, keepdims=True)
    )
    grad_hidden = (cotangent_rows.astype(jnp.float32) + inv_std * correction).astype(jnp.bfloat16)
    gh_half = own_half(grad_hidden, core)
    gh_half_other = swap(own_half(grad_hidden, 1 - core), "dp", 0)
    conv_share = (
        dot_columns(conv_left, gh_half) + dot_columns(conv_left_other, gh_half_other)
    ).astype(jnp.bfloat16)

    conv_sum, qkv_sum, proj_sum = sum_over_devices(
        [by_owner(conv_share, 3), by_owner(qkv_share, 1), by_owner(proj_share, 1)], grad_scale
    )

    grad_four = grad_hidden.reshape(tm_count, half, loc, width)
    rim_after = from_behind(grad_four[:, 0], "tm", -1)
    grad_next = jnp.concatenate([grad_four[:, 1:], rim_after[:, None]], axis=1)
    grad_even = dot_rows_t(grad_hidden, tap_one).astype(jnp.bfloat16)
    grad_odd = (dot_rows_t(grad_hidden, tap_two) + dot_rows_t(as_rows(grad_next), tap_zero)).astype(
        jnp.bfloat16
    )
    by_frame = (tm_count, half, loc, width)
    input_grad = jnp.transpose(
        jnp.stack([grad_even.reshape(by_frame), grad_odd.reshape(by_frame)], axis=0),
        (2, 0, 1, 3, 4),
    ).reshape(latents.shape)

    def assembled(gathered):
        ordered = jnp.transpose(gathered, (2, 3, 1, 0, 4))
        return ordered.reshape(ordered.shape[0] * ordered.shape[1], -1)

    conv_grad = assembled(conv_sum)
    qkv_grad = assembled(qkv_sum)
    proj_grad = assembled(proj_sum)
    return (input_grad, conv_grad, qkv_grad, proj_grad)


def solution(mesh):
    return jax.shard_map(
        local,
        mesh=mesh,
        in_specs=(P("dp", "tm", None, None), P(), P(), P(), P("dp", "tm", None, None)),
        out_specs=(P("dp", "tm", None, None), P("tm", None), P("tm", None), P("tm", None)),
        check_vma=False,
    )
```
